32 devices in a mesh: clips: 2 (over y), tiles: 4 (over z), frames: 2 (over x), chan: 2 (over core).
Axes of the slice: x: 2, y: 2, z: 4, core: 2. Of those that a mesh axis runs over, the one named last changes fastest.
Arguments:
- lr_feats: bfloat16 [8, 2, 64, 32, 128], P('clips', 'frames', 'chan', 'tiles'), parts along dimension 0, may hold values from -6 to 6
- flow_prev: int32 [8, 2, 4, 2], P('clips', None, 'tiles'), parts along dimension 0, may hold values from -8 to 8, as said below
- flow_second: int32 [8, 2, 4, 2], P('clips', None, 'tiles'), parts along dimension 0, may hold values from -8 to 8, as said below
- w_join: bfloat16 [9, 64, 192], P(None, 'chan'), may hold values from -0.15625 to 0.15625
- b_join: float32 [64], P('chan'), may hold values from -3 to 3
- w_first: bfloat16 [1, 9, 64, 64], P(None, None, 'chan'), may hold values from -0.25 to 0.25
- b_first: float32 [1, 64], P(None, 'chan'), may hold values from -3 to 3
- w_second: bfloat16 [1, 9, 64, 64], P(None, None, 'chan'), may hold values from -0.25 to 0.25
- b_second: float32 [1, 64], P(None, 'chan'), may hold values from -3 to 3
Outputs:
- hidden: bfloat16 [8, 2, 64, 32, 128], P('clips', 'frames', 'chan', 'tiles'), parts along dimension 0
The draws below stay inside these ranges and needn't reach their ends.
There are 2 independent parts, one for each index of `clips`. The reference program is written for one: setup_inputs(seed, part) draws one part's arguments, and reference() takes and returns one part's arrays. A program takes and returns all parts, laid end to end along the dimension named above; an argument that names none is the same for every part. Nothing has to cross between parts.
Inputs may be any that keep to these rules, and one draw needn't show every extreme that they name: `flow_prev`: both entries (dy, dx) of every block lie in the range; +8 and -8 each occur in every draw. `flow_second`: both entries (dy, dx) of every block lie in the range; +8 and -8 each occur in every draw.
All inputs are finite; a program needn't handle non-finite values.
Results may differ from the reference program's by a relative error of at most 0.012.
Values may be sent and summed in bfloat16 or wider, within the bound.
No kernel may reach another device: no remote copies, remote signals or barrier semaphores. Data moves between devices by JAX's collectives and lax.ppermute only.
A program may use at most 64 MiB of HBM per device.

```python
import jax
import jax.numpy as jnp
from jax import lax

C = 64
RES = 1
BH = 8
COLS = 128
TR = 8
SEGS = 4
FRAMES = 2
ROWS = 32
NBLK = 4


def draw_offsets(key, salt_value):
    inner_key = jax.random.fold_in(key, salt_value)
    key_first, key_second, key_third = jax.random.split(inner_key, 3)
    count_all = SEGS * FRAMES * NBLK
    values = jax.random.randint(key_first, (count_all, 2), -TR, TR + 1, dtype=jnp.int32)
    top_index = jax.random.randint(key_second, (), 0, count_all, dtype=jnp.int32)
    low_index = jax.random.randint(key_third, (), 0, count_all, dtype=jnp.int32)
    values = values.at[top_index, 0].set(TR)
    values = values.at[low_index, 1].set(-TR)
    return values.reshape(SEGS, FRAMES, NBLK, 2)


def draw_flow_prev(key, part):
    return draw_offsets(key, 11)


def draw_flow_second(key, part):
    return draw_offsets(key, 23)


def block_levels(own_key, dims, shards, smallest, largest):
    loudness, own = 1.0, jax.random.fold_in(own_key, 6)
    for position, parts in shards:
        heights = jnp.exp(jax.random.uniform(jax.random.fold_in(own, position), (parts,), jnp.float32, smallest / len(shards), largest / len(shards)))
        loudness = loudness * jnp.repeat(heights, dims[position] // parts).reshape([-1 if axis == position else 1 for axis in range(len(dims))])
    return loudness


def normal_values(rng, extent, deviation, bound, cuts=(), kind=jnp.bfloat16):
    result = jax.random.normal(rng, extent, jnp.float32) * deviation
    if len(cuts) > 0:
        result = block_levels(rng, extent, cuts, -0.22, 0.18) * result
    return jnp.clip(result, min=-bound, max=bound).astype(kind)


def setup_inputs(seed: int = 0, part: int = 0) -> dict:
    key_of = jax.random.split(jax.random.key(seed), 10)
    own_keys = jax.random.split(jax.random.fold_in(key_of[9], part), 10)
    lr_feats = normal_values(own_keys[0], (SEGS, FRAMES, C, ROWS, COLS), 1.0, 6.0, ((1, 2), (2, 2), (3, 4)))
    flow_prev = draw_flow_prev(jax.random.fold_in(jax.random.fold_in(key_of[9], part), 71), part)
    flow_second = draw_flow_second(jax.random.fold_in(jax.random.fold_in(key_of[9], part), 71), part)
    w_join = normal_values(key_of[3], (9, C, 3 * C), (27 * C) ** -0.5, 0.15625, ((1, 2),))
    b_join = normal_values(key_of[4], (C,), 0.5, 3.0, ((0, 2),), jnp.float32)
    w_first = normal_values(key_of[5], (RES, 9, C, C), (9 * C) ** -0.5, 0.25, ((2, 2),))
    b_first = normal_values(key_of[6], (RES, C), 0.5, 3.0, ((1, 2),), jnp.float32)
    w_second = normal_values(key_of[7], (RES, 9, C, C), (9 * C) ** -0.5, 0.25, ((2, 2),))
    b_second = normal_values(key_of[8], (RES, C), 0.5, 3.0, ((1, 2),), jnp.float32)
    return dict(lr_feats=lr_feats, flow_prev=flow_prev, flow_second=flow_second, w_join=w_join, b_join=b_join, w_first=w_first, b_first=b_first, w_second=w_second, b_second=b_second)


def shift_blocks(feature, offsets):
    channels = feature.shape[0]
    col_count = feature.shape[2]
    padded = jnp.pad(feature, ((0, 0), (TR, TR), (TR, TR)))

    def take_block(block_number):
        start_row = (TR + block_number * BH + offsets[block_number, 0]).astype(jnp.int32)
        start_col = (TR + offsets[block_number, 1]).astype(jnp.int32)
        return lax.dynamic_slice(padded, (jnp.zeros((), jnp.int32), start_row, start_col), (channels, BH, col_count))

    pieces = jax.vmap(take_block)(jnp.arange(NBLK, dtype=jnp.int32))
    return jnp.transpose(pieces, (1, 0, 2, 3)).reshape(channels, NBLK * BH, col_count)


def convolve(inputs, weights, bias_vec):
    in_count, row_count, col_count = inputs.shape
    padded = jnp.pad(inputs, ((0, 0), (1, 1), (1, 1)))
    total_sum = jnp.zeros((weights.shape[1], row_count * col_count), jnp.float32)
    for tap_index in range(9):
        tap_row = tap_index // 3
        tap_col = tap_index % 3
        window = padded[:, tap_row:tap_row + row_count, tap_col:tap_col + col_count].reshape(in_count, row_count * col_count)
        total_sum = total_sum + jnp.dot(weights[tap_index], window, preferred_element_type=jnp.float32)
    return total_sum.reshape(-1, row_count, col_count) + bias_vec[:, None, None]


def refine(current, warped_one, warped_two, w_join, b_join, w_first, b_first, w_second, b_second):
    stacked = jnp.concatenate([current, warped_one, warped_two], axis=0)
    joined_sum = convolve(stacked, w_join, b_join)
    joined_state = jnp.where(joined_sum > 0, joined_sum, 0.1 * joined_sum).astype(jnp.bfloat16)
    for block_index in range(RES):
        inner_act = jnp.maximum(convolve(joined_state, w_first[block_index], b_first[block_index]), 0.0).astype(jnp.bfloat16)
        joined_state = (joined_state.astype(jnp.float32) + convolve(inner_act, w_second[block_index], b_second[block_index])).astype(jnp.bfloat16)
    return joined_state


def reference(lr_feats, flow_prev, flow_second, w_join, b_join, w_first, b_first, w_second, b_second):
    zero_feat = jnp.zeros(lr_feats.shape[2:], lr_feats.dtype)
    all_segments = []
    for segment in range(SEGS):
        older_feat = zero_feat
        newer_feat = zero_feat
        frame_list = []
        for frame_index in range(FRAMES):
            warped_one = shift_blocks(newer_feat, flow_prev[segment, frame_index])
            warped_two = shift_blocks(older_feat, flow_second[segment, frame_index])
            fresh_state = refine(lr_feats[segment, frame_index], warped_one, warped_two, w_join, b_join, w_first, b_first, w_second, b_second)
            frame_list.append(fresh_state)
            older_feat = newer_feat
            newer_feat = fresh_state
        all_segments.append(jnp.stack(frame_list))
    return jnp.stack(all_segments)
```

```python
import functools

import jax
import jax.numpy as jnp
from jax import lax
from jax.experimental import pallas as pl
from jax.experimental.pallas import tpu as pltpu
from jax.sharding import PartitionSpec as P

TAPS = 3
CHUNK = 8


def hop(array, axis, step):
    count = lax.axis_size(axis)
    if step % count == 0:
        return array
    return lax.ppermute(array, axis, [(i, (i + step) % count) for i in range(count)])


def moved(value, step):
    cols = value.shape[1]
    lane = lax.broadcasted_iota(jnp.int32, value.shape, 1)
    rolled = pltpu.roll(value, lax.rem(cols - step, cols), 1)
    return jnp.where((lane + step >= 0) & (lane + step < cols), rolled, 0.0)


def fan(value):
    taps = [moved(value, -1), value, moved(value, 1)]
    return [tap.astype(jnp.bfloat16) for tap in taps]


def recurrence(sizes, place, flows, w_join, w_first, w_second, b_join, b_first, b_second, *rest):
    frames, tiles, chans, groups, span, count, part, depth, cols = sizes
    n_blocks = frames * tiles * chans
    blocks, rest = rest[:n_blocks], rest[n_blocks:]
    outs, rest = rest[:groups], rest[groups:]
    slots, stage, features, sources, joined, history, arrived = rest
    channels = part * chans
    rows = tiles * depth
    tile, frame_here, chan = place[0], place[1], place[2]
    kept = history.shape[0]
    top = depth + 1

    def copies(segment, shift):
        for index in range(tiles * chans):
            yield pltpu.make_async_copy(
                blocks[shift * tiles * chans + index].at[segment],
                slots.at[shift % 2, index],
                arrived.at[shift % 2, index],
            )

    def load(segment):
        for copy in copies(segment, 0):
            copy.start()
        for shift in range(frames):
            if shift + 1 < frames:
                for copy in copies(segment, shift + 1):
                    copy.start()
            frame = lax.rem(frame_here - shift + frames, frames)
            pending = list(copies(segment, shift))
            for index in range(tiles * chans):
                source_tile = lax.rem(tile - index // chans + tiles, tiles)
                source_chan = lax.rem(chan - index % chans + chans, chans)
                pending[index].wait()
                block = slots[shift % 2, index, :part].astype(jnp.float32)
                stage[index] = block.reshape(part * depth, cols)
                first = pl.multiple_of(source_chan * part, part)
                for row in range(depth):
                    value = stage[index, pl.ds(row, part, stride=depth), :]
                    features[frame, source_tile * depth + row, pl.ds(first, part), :] = (
                        value.astype(jnp.bfloat16)
                    )

    def convolve(inputs, weights, bias, emit):
        def step(chunk, carried):
            above, here = carried
            start = chunk * CHUNK
            slabs = [
                jnp.concatenate([ref[start + row + 1] for ref in inputs], axis=0)
                for row in range(CHUNK)
            ]
            partial = jnp.dot(
                weights, jnp.concatenate(slabs, axis=1), preferred_element_type=jnp.float32
            )
            for row in range(CHUNK):
                one = partial[:, row * cols : (row + 1) * cols]
                emit(start + row, above + one[2 * channels :])
                above = here + one[channels : 2 * channels]
                here = bias + one[:channels]
            return above, here

        above, _ = lax.fori_loop(0, rows // CHUNK, step, (bias, bias))
        emit(rows, above)

    def spread(ref, slot, value):
        for tap, shifted in enumerate(fan(value)):
            ref[slot, tap * channels : (tap + 1) * channels, :] = shifted

    def displace(held, target, segment, field):
        def one_block(block, _):
            origin = lax.rem(tile - block + tiles, tiles)
            down = flows[segment, origin, field]
            right = flows[segment, origin, field + 1]
            for row in range(depth):
                at = block * depth + row
                value = held[top + at + down].astype(jnp.float32)
                spread(target, at + 1, moved(value, right))
            return 0

        lax.fori_loop(0, tiles, one_block, 0)

    for index in range(kept):
        history[index, :top] = jnp.zeros((top, channels, cols), jnp.bfloat16)
        history[index, top + rows :] = jnp.zeros((depth, channels, cols), jnp.bfloat16)

    for segment in range(count):
        load(segment)
        for frame in range(frames):
            inputs = [sources.at[0]]

            def spread_own(row, _, frame=frame):
                spread(sources.at[0], row + 1, features[frame, row].astype(jnp.float32))
                return 0

            lax.fori_loop(0, rows, spread_own, 0)
            for back, field in ((1, 2 * frame), (2, 2 * (frames + frame))):
                if frame >= back:
                    displace(history.at[(frame - back) % kept], sources.at[back], segment, field)
                    inputs.append(sources.at[back])
            width = TAPS * channels * len(inputs)
            new = history.at[frame % kept]

            def emit_join(slot, total):
                spread(joined, slot, jnp.where(total > 0, total, 0.1 * total))

            def emit_inner(slot, total):
                spread(sources.at[0], slot, jnp.maximum(total, 0.0))

            def emit_second(slot, total, new=new):
                state = joined[slot, channels : 2 * channels, :].astype(jnp.float32) + total
                new[top - 1 + slot] = state.astype(jnp.bfloat16)

            convolve(inputs, w_join[:, :width], b_join[...], emit_join)
            convolve([joined], w_first[...], b_first[...], emit_inner)
            convolve([sources.at[0]], w_second[...], b_second[...], emit_second)
            new[top - 1] = jnp.zeros((channels, cols), jnp.bfloat16)

            @pl.when(frame_here == frame)
            def _(segment=segment, new=new):
                first = pl.multiple_of(chan * part, part)
                for turn in range(groups):
                    target = lax.rem(tile + turn * span, tiles)
                    for row in range(depth):
                        value = new[top + target * depth + row, pl.ds(first, part), :]
                        stage[turn, pl.ds(row, part, stride=depth), :] = value.astype(jnp.float32)
                    whole = stage[turn].reshape(part, depth, cols)
                    outs[turn][segment] = whole.astype(jnp.bfloat16)


def shards(lr_feats, flow_prev, flow_second, w_join, b_join, w_first, b_first, w_second, b_second):
    segments, _, part, depth, cols = lr_feats.shape
    frames, tiles, chans = (lax.axis_size(name) for name in ("frames", "tiles", "chan"))
    tile, frame, chan = (lax.axis_index(name) for name in ("tiles", "frames", "chan"))
    span = max(1, tiles // segments)
    groups = tiles // span
    count = segments // groups
    channels = part * chans

    offsets = jnp.concatenate(
        [flow.reshape(segments, frames * 2) for flow in (flow_prev, flow_second)], axis=1
    )
    fields = offsets.shape[1]
    plane = jnp.pad(offsets.astype(jnp.bfloat16), ((0, 0), (0, cols - fields)))
    plane = jnp.broadcast_to(plane[:, None, None], (segments, 1, depth, cols))
    payload = jnp.concatenate([lr_feats[:, 0], plane], axis=1)

    def for_tile(index):
        return lax.dynamic_slice_in_dim(payload, lax.rem(index, tiles) // span * count, count, 0)

    own = [hop(for_tile(tile + shift), "tiles", shift) for shift in range(tiles)]
    blocks = []
    for turn in range(frames):
        for shift in range(tiles):
            block = hop(own[shift], "frames", turn)
            blocks += [hop(block, "chan", side) for side in range(chans)]
    flows = jnp.stack([block[:, part, 0, :fields] for block in own], axis=1).astype(jnp.int32)

    def gathered(array, dim):
        pieces = [hop(array, "chan", side) for side in range(chans)]
        if chans == 2:
            low = jnp.where(chan == 0, pieces[0], pieces[1])
            high = jnp.where(chan == 0, pieces[1], pieces[0])
            return jnp.concatenate([low, high], axis=dim)
        return lax.all_gather(array, "chan", axis=dim, tiled=True)

    w_all = gathered(jnp.concatenate([w_join, w_first[0], w_second[0]], axis=2), 1)
    b_all = gathered(jnp.stack([b_join, b_first[0], b_second[0]]), 1)

    def arranged(weights):
        inputs = weights.shape[2] // channels
        split = weights.reshape(TAPS, TAPS, channels, inputs, channels)
        return split.transpose(0, 2, 3, 1, 4).reshape(TAPS * channels, inputs * TAPS * channels)

    w_sizes = (w_join.shape[2], w_first.shape[3], w_second.shape[3])
    edges = (w_sizes[0], w_sizes[0] + w_sizes[1])
    weights = [arranged(part_w) for part_w in jnp.split(w_all, edges, axis=2)]
    biases = [jnp.broadcast_to(row[:, None], (channels, cols)) for row in b_all]

    rows = tiles * depth
    kept = min(frames, 3)
    sizes = (frames, tiles, chans, groups, span, count, part, depth, cols)
    vmem = pl.BlockSpec(memory_space=pltpu.VMEM)
    smem = pl.BlockSpec(memory_space=pltpu.SMEM)
    block_shape = (part + 1, depth, cols)
    wide = TAPS * channels
    outs = pl.pallas_call(
        functools.partial(recurrence, sizes),
        out_shape=[jax.ShapeDtypeStruct((count, part, depth, cols), jnp.bfloat16)] * groups,
        in_specs=[smem, smem] + [vmem] * 6 + [pl.BlockSpec(memory_space=pl.ANY)] * len(blocks),
        out_specs=[vmem] * groups,
        scratch_shapes=[
            pltpu.VMEM((2, tiles * chans) + block_shape, jnp.bfloat16),
            pltpu.VMEM((tiles * chans, part * depth, cols), jnp.float32),
            pltpu.VMEM((frames, rows, channels, cols), jnp.bfloat16),
            pltpu.VMEM((3, rows + 1, wide, cols), jnp.bfloat16),
            pltpu.VMEM((rows + 1, wide, cols), jnp.bfloat16),
            pltpu.VMEM((kept, rows + 2 * depth + 1, channels, cols), jnp.bfloat16),
            pltpu.SemaphoreType.DMA((2, tiles * chans)),
        ],
    )(jnp.stack([tile, frame, chan]).astype(jnp.int32), flows, *weights, *biases, *blocks)

    done = jnp.stack([hop(out, "tiles", turn * span) for turn, out in enumerate(outs)])
    turn_of = lax.rem(tile // span - jnp.arange(groups) + groups, groups)
    return jnp.take(done, turn_of, axis=0).reshape(segments, 1, part, depth, cols)


def solution(mesh):
    in_specs = (
        P("clips", "frames", "chan", "tiles", None),
        P("clips", None, "tiles", None),
        P("clips", None, "tiles", None),
        P(None, "chan", None),
        P("chan"),
        P(None, None, "chan", None),
        P(None, "chan"),
        P(None, None, "chan", None),
        P(None, "chan"),
    )
    out_specs = P("clips", "frames", "chan", "tiles", None)
    return jax.shard_map(shards, mesh=mesh, in_specs=in_specs, out_specs=out_specs, check_vma=False)
```

```python
import functools

import jax
import jax.numpy as jnp
from jax import lax
from jax.experimental import pallas as pl
from jax.experimental.pallas import tpu as pltpu
from jax.sharding import PartitionSpec as P

TAPS = 3
UNROLL = 4
VMEM = pl.BlockSpec(memory_space=pltpu.VMEM)
SMEM = pl.BlockSpec(memory_space=pltpu.SMEM)
ANY = pl.BlockSpec(memory_space=pl.ANY)


def hop(array, axis, step):
    count = lax.axis_size(axis)
    if step % count == 0:
        return array
    return lax.ppermute(array, axis, [(i, (i + step) % count) for i in range(count)])


def split_of(segments, tiles):
    span = max(1, tiles // segments)
    groups = tiles // span
    return span, groups, segments // groups


def pack(lr_feats, *rest):
    outs, stage = rest[:-1], rest[-1]
    segments, _, part, depth, cols = lr_feats.shape
    tiles = len(outs)
    span, groups, count = split_of(segments, tiles)
    tile = lax.axis_index("tiles")
    for shift, out in enumerate(outs):
        first = lax.rem(tile + shift, tiles) // span * count
        for index in range(count):
            block = lr_feats[first + index, 0].astype(jnp.float32)
            slot = shift * count + index
            stage[slot] = block.reshape(part * depth, cols)
            for row in range(depth):
                value = stage[slot, pl.ds(row, part, stride=depth), :]
                out[index, row] = value.astype(jnp.bfloat16)


def unpack(*refs):
    blocks, out, stage = refs[:-2], refs[-2], refs[-1]
    segments, _, part, depth, cols = out.shape
    groups, count = len(blocks), segments // len(blocks)
    span = lax.axis_size("tiles") // groups
    tile = lax.axis_index("tiles")
    for turn, block in enumerate(blocks):
        first = lax.rem(tile // span - turn + groups, groups) * count
        for index in range(count):
            slot = turn * count + index
            for row in range(depth):
                value = block[index, row].astype(jnp.float32)
                stage[slot, pl.ds(row, part, stride=depth), :] = value
            whole = stage[slot].reshape(part, depth, cols)
            out[first + index, 0] = whole.astype(jnp.bfloat16)


def arrange(widths, *refs):
    chans = (len(refs) - 4) // 2
    weights, biases, outs = refs[:chans], refs[chans : 2 * chans], refs[2 * chans :]
    part = weights[0].shape[1]
    channels = part * chans
    chan = lax.axis_index("chan")
    cols = outs[3].shape[2]
    for side in range(chans):
        at = lax.rem(chan - side + chans, chans) * part
        low = 0
        for width, out in zip(widths, outs):
            for row in range(TAPS):
                pieces = [
                    weights[side][TAPS * row + col, :, low + source : low + source + channels]
                    for source in range(0, width, channels)
                    for col in range(TAPS)
                ]
                place = pl.multiple_of(row * channels + at, part)
                out[pl.ds(place, part), :] = jnp.concatenate(pieces, axis=1)
            low += width
        diagonal = lax.broadcasted_iota(jnp.int32, (part, part), 0) == lax.broadcasted_iota(
            jnp.int32, (part, part), 1
        )
        for index in range(len(widths)):
            spread = jnp.broadcast_to(biases[side][index : index + 1, :], (part, part))
            column = jnp.sum(jnp.where(diagonal, spread, 0.0), axis=1, keepdims=True)
            outs[3][index, pl.ds(pl.multiple_of(at, part), part), :] = jnp.broadcast_to(
                column, (part, cols)
            )


def moved(value, step):
    cols = value.shape[1]
    lane = lax.broadcasted_iota(jnp.int32, value.shape, 1)
    rolled = pltpu.roll(value, lax.rem(cols - step, cols), 1)
    return jnp.where((lane + step >= 0) & (lane + step < cols), rolled, jnp.zeros_like(rolled))


def taps(value):
    return jnp.concatenate([moved(value, -1), value, moved(value, 1)], axis=0)


def recurrence(sizes, *refs):
    frames, tiles, chans, segments, part, depth, cols = sizes
    span, groups, count = split_of(segments, tiles)
    n_blocks = frames * tiles * chans
    flows, refs = refs[:tiles], refs[tiles:]
    (w_join, w_first, w_second, biases), refs = refs[:4], refs[4:]
    blocks, refs = refs[:n_blocks], refs[n_blocks:]
    outs, refs = refs[:groups], refs[groups:]
    table, features, joined, inner, history, arrived, left = refs
    channels = part * chans
    rows = tiles * depth
    tile, frame_here, chan = (lax.axis_index(name) for name in ("tiles", "frames", "chan"))
    first_segment = tile // span * count
    kept = history.shape[0]
    top = depth + 1

    def copy_in(segment, shift, index):
        frame = lax.rem(frame_here - shift + frames, frames)
        source_tile = lax.rem(tile - index // chans + tiles, tiles)
        source_chan = lax.rem(chan - index % chans + chans, chans)
        target = features.at[
            frame,
            pl.ds(source_tile * depth, depth),
            pl.ds(pl.multiple_of(source_chan * part, part), part),
        ]
        source = blocks[shift * tiles * chans + index].at[segment]
        return pltpu.make_async_copy(source, target, arrived.at[shift, index])

    def every_copy(segment):
        for shift in range(frames):
            for index in range(tiles * chans):
                yield copy_in(segment, shift, index)

    def convolve(inputs, weights, bias, emit):
        def step(block, carried):
            above, here = carried
            slabs = [
                jnp.concatenate([taps(load(block, row)) for load in inputs], axis=0)
                for row in range(depth)
            ]
            partial = jnp.dot(
                weights, jnp.concatenate(slabs, axis=1), preferred_element_type=jnp.float32
            )
            for row in range(depth):
                one = partial[:, row * cols : (row + 1) * cols]
                emit(block * depth + row, above + one[2 * channels :])
                above = here + one[channels : 2 * channels]
                here = bias + one[:channels]
            return above, here

        unroll = UNROLL if tiles % UNROLL == 0 else 1
        above, _ = lax.fori_loop(0, tiles, step, (bias, bias), unroll=unroll)
        emit(rows, above)

    def stored(ref):
        return lambda block, row: ref[block * depth + row + 1]

    def displaced(held, segment, field):
        def load(block, row):
            down = table[segment, block, field]
            right = table[segment, block, field + 1]
            return moved(held[top + block * depth + row + down], right)

        return load

    for segment in range(count):
        for copy in every_copy(segment):
            copy.start()
        if segment == 0:
            for shift in range(tiles):
                for index in range(count):
                    for field in range(4 * frames):
                        origin = lax.rem(tile - shift + tiles, tiles)
                        table[index, origin, field] = flows[shift][first_segment + index, field]
            for index in range(kept):
                history[index, :top] = jnp.zeros((top, channels, cols), jnp.bfloat16)
                history[index, top + rows :] = jnp.zeros((depth, channels, cols), jnp.bfloat16)
        for copy in every_copy(segment):
            copy.wait()
        for frame in range(frames):
            inputs = [lambda block, row, frame=frame: features[frame, block * depth + row]]
            for back, field in ((1, 2 * frame), (2, 2 * (frames + frame))):
                if frame >= back:
                    inputs.append(displaced(history.at[(frame - back) % kept], segment, field))
            width = TAPS * channels * len(inputs)
            new = history.at[frame % kept]

            def emit_join(slot, total):
                joined[slot] = jnp.where(total > 0, total, 0.1 * total).astype(jnp.bfloat16)

            def emit_inner(slot, total):
                inner[slot] = jnp.maximum(total, 0.0).astype(jnp.bfloat16)

            def emit_second(slot, total, new=new):
                state = joined[slot].astype(jnp.float32) + total
                new[top - 1 + slot] = state.astype(jnp.bfloat16)

            convolve(inputs, w_join[:, :width], biases[0], emit_join)
            convolve([stored(joined)], w_first[...], biases[1], emit_inner)
            convolve([stored(inner)], w_second[...], biases[2], emit_second)
            new[top - 1] = jnp.zeros((channels, cols), jnp.bfloat16)

            @pl.when(frame_here == frame)
            def _(segment=segment, new=new):
                sends = []
                for turn in range(groups):
                    target = lax.rem(tile + turn * span, tiles)
                    source = new.at[
                        pl.ds(top + target * depth, depth),
                        pl.ds(pl.multiple_of(chan * part, part), part),
                    ]
                    sends.append(
                        pltpu.make_async_copy(source, outs[turn].at[segment], left.at[turn])
                    )
                for send in sends:
                    send.start()
                for send in sends:
                    send.wait()


def shards(lr_feats, flow_prev, flow_second, w_join, b_join, w_first, b_first, w_second, b_second):
    segments, _, part, depth, cols = lr_feats.shape
    frames, tiles, chans = (lax.axis_size(name) for name in ("frames", "tiles", "chan"))
    span, groups, count = split_of(segments, tiles)
    channels = part * chans
    rows = tiles * depth
    kept = min(frames, 3)
    block = jax.ShapeDtypeStruct((count, depth, part, cols), jnp.bfloat16)

    packed = pl.pallas_call(
        pack,
        out_shape=[block] * tiles,
        in_specs=[VMEM],
        out_specs=[VMEM] * tiles,
        scratch_shapes=[pltpu.VMEM((tiles * count, part * depth, cols), jnp.float32)],
    )(lr_feats)
    own = [hop(packed[shift], "tiles", shift) for shift in range(tiles)]
    blocks = []
    for turn in range(frames):
        for shift in range(tiles):
            arrived = hop(own[shift], "frames", turn)
            blocks += [hop(arrived, "chan", side) for side in range(chans)]

    offsets = [flow.reshape(segments, frames * 2) for flow in (flow_prev, flow_second)]
    offsets, _ = lax.optimization_barrier((jnp.concatenate(offsets, axis=1), own[1]))
    flows = [hop(offsets, "tiles", shift) for shift in range(tiles)]

    w_own = jnp.concatenate([w_join, w_first[0], w_second[0]], axis=2)
    b_own = jnp.stack([b_join, b_first[0], b_second[0]])
    widths = (w_join.shape[2], w_first.shape[3], w_second.shape[3])
    arranged = pl.pallas_call(
        functools.partial(arrange, widths),
        out_shape=[
            jax.ShapeDtypeStruct((TAPS * channels, TAPS * width), jnp.bfloat16) for width in widths
        ]
        + [jax.ShapeDtypeStruct((len(widths), channels, cols), jnp.float32)],
        in_specs=[VMEM] * (2 * chans),
        out_specs=[VMEM] * 4,
    )(*[hop(w_own, "chan", s) for s in range(chans)], *[hop(b_own, "chan", s) for s in range(chans)])

    outs = pl.pallas_call(
        functools.partial(recurrence, (frames, tiles, chans, segments, part, depth, cols)),
        out_shape=[block] * groups,
        in_specs=[SMEM] * tiles + [VMEM] * 4 + [ANY] * len(blocks),
        out_specs=[ANY] * groups,
        scratch_shapes=[
            pltpu.SMEM((count, tiles, 4 * frames), jnp.int32),
            pltpu.VMEM((frames, rows, channels, cols), jnp.bfloat16),
            pltpu.VMEM((rows + 1, channels, cols), jnp.bfloat16),
            pltpu.VMEM((rows + 1, channels, cols), jnp.bfloat16),
            pltpu.VMEM((kept, rows + 2 * depth + 1, channels, cols), jnp.bfloat16),
            pltpu.SemaphoreType.DMA((frames, tiles * chans)),
            pltpu.SemaphoreType.DMA((groups,)),
        ],
    )(*flows, *arranged, *blocks)

    return pl.pallas_call(
        unpack,
        out_shape=jax.ShapeDtypeStruct(lr_feats.shape, lr_feats.dtype),
        in_specs=[VMEM] * groups,
        out_specs=VMEM,
        scratch_shapes=[pltpu.VMEM((segments, part * depth, cols), jnp.float32)],
    )(*[hop(out, "tiles", turn * span) for turn, out in enumerate(outs)])


def solution(mesh):
    in_specs = (
        P("clips", "frames", "chan", "tiles", None),
        P("clips", None, "tiles", None),
        P("clips", None, "tiles", None),
        P(None, "chan", None),
        P("chan"),
        P(None, None, "chan", None),
        P(None, "chan"),
        P(None, None, "chan", None),
        P(None, "chan"),
    )
    out_specs = P("clips", "frames", "chan", "tiles", None)
    return jax.shard_map(shards, mesh=mesh, in_specs=in_specs, out_specs=out_specs, check_vma=False)
```

```python
import functools
import math

import jax
import jax.numpy as jnp
from jax import lax
from jax.experimental import pallas as pl
from jax.experimental.pallas import tpu as pltpu
from jax.sharding import PartitionSpec as P


TAPS = 3
LANES = 128
TAIL = 8
PIECES = 3
UNROLL = 4
SPARE = 4 * 2**20
VMEM = pl.BlockSpec(memory_space=pltpu.VMEM)
HBM = pl.BlockSpec(memory_space=pltpu.HBM)


def partner(index, shift, count):
    return (index + shift) % count if isinstance(index, int) else lax.rem(index + shift, count)


def origin(index, shift, count):
    return lax.rem(index + count - shift, count)


def hop(array, axis, shift, stride=1):
    count = lax.axis_size(axis) // stride
    if shift == 0:
        return array
    pairs = [
        (i * stride + j, partner(i, shift, count) * stride + j)
        for i in range(count)
        for j in range(stride)
    ]
    return lax.ppermute(array, axis, pairs)


def ranked(count):
    return list(range(1, count))


def in_hbm(*arrays):
    return tuple(pltpu.with_memory_space_constraint(array, pltpu.HBM) for array in arrays)


def call(kernel, operands, out_shape, scratch, in_specs, out_specs):
    shapes = jax.tree.leaves((operands, out_shape))
    held = sum(
        shape.size * shape.dtype.itemsize
        for shape in shapes
    ) + sum(
        math.prod(item.shape) * jnp.dtype(item.dtype).itemsize
        for item in scratch
        if item.memory_space == pltpu.VMEM
    )
    return pl.pallas_call(
        kernel,
        out_shape=out_shape,
        in_specs=in_specs,
        out_specs=out_specs,
        scratch_shapes=scratch,
        compiler_params=pltpu.CompilerParams(vmem_limit_bytes=held + SPARE),
    )(*operands)


def split_of(segments, tiles):
    span = max(1, tiles // segments)
    groups = tiles // span
    return span, groups, segments // groups


def starts_of(widths):
    starts, at = [], 0
    for width in widths:
        starts.append(at)
        at += -(-TAPS * width // LANES) * LANES
    return starts + [at]


def pack(lr_feats, *rest):
    flows, rest = rest[:2], rest[2:]
    outs, rest = rest[:-5], rest[-5:]
    held, table_prev, table_second, stage, came = rest
    segments, _, part, depth, cols = lr_feats.shape
    frames = flows[0].shape[0]
    tiles = len(outs)
    span, _, count = split_of(segments, tiles)
    tile = lax.axis_index("tiles")
    tables = (table_prev, table_second)
    fetches = [
        pltpu.make_async_copy(flow, table, came.at[len(outs) * count + index])
        for index, (flow, table) in enumerate(zip(flows, tables))
    ]
    order = ranked(tiles) + [0]

    def first_of(shift):
        return partner(tile, shift, tiles) // span * count

    loads = {}
    for shift in order:
        for index in range(count):
            slot = shift * count + index
            loads[slot] = pltpu.make_async_copy(
                lr_feats.at[first_of(shift) + index, 0], held.at[slot], came.at[slot]
            )
            loads[slot].start()
    for fetch in fetches:
        fetch.start()
    lane = lax.broadcasted_iota(jnp.int32, (TAIL, cols), 1)
    for shift in order:
        for index in range(count):
            slot = shift * count + index
            loads[slot].wait()
            stage[slot] = held[slot].astype(jnp.float32).reshape(part * depth, cols)
            for row in range(depth):
                value = stage[slot, pl.ds(row, part, stride=depth), :]
                outs[shift][index, row * part : (row + 1) * part] = value.astype(jnp.bfloat16)
    for fetch in fetches:
        fetch.wait()
    for shift in order:
        for index in range(count):
            tail = jnp.zeros((TAIL, cols), jnp.int32)
            for which, table in enumerate(tables):
                for frame in range(frames):
                    for entry in range(2):
                        at = (which * frames + frame) * 2 + entry
                        number = table[frame, 0, entry, first_of(shift) + index]
                        tail = jnp.where(lane == at, number, tail)
            outs[shift][index, part * depth :] = tail.astype(jnp.float32).astype(jnp.bfloat16)


def unpack(*refs):
    blocks, out, left = refs[:-2], refs[-2], refs[-1]
    groups = len(blocks)
    count = out.shape[0] // groups
    span = lax.axis_size("tiles") // groups
    tile = lax.axis_index("tiles")
    copies = []
    for turn, block in enumerate(blocks):
        first = origin(tile // span, turn, groups) * count
        for index in range(count):
            copies.append(
                pltpu.make_async_copy(
                    block.at[index], out.at[first + index, 0], left.at[turn * count + index]
                )
            )
    for copy in copies:
        copy.start()
    for copy in copies:
        copy.wait()


def arrange(widths, *refs):
    count = len(widths)
    sources, out, rest = refs[: 2 * count], refs[2 * count], refs[2 * count + 1 :]
    copies = [
        pltpu.make_async_copy(source, held, rest[-1].at[index])
        for index, (source, held) in enumerate(zip(sources, rest))
    ]
    for copy in copies:
        copy.start()
    for copy in copies:
        copy.wait()
    weights, biases = rest[:count], rest[count : 2 * count]
    part = out.shape[0] // TAPS
    *starts, end = starts_of(widths)
    channels = min(widths)
    for weight, width, start in zip(weights, widths, starts):
        for row in range(TAPS):
            pieces = [
                weight[TAPS * row + col, :, source : source + channels]
                for source in range(0, width, channels)
                for col in range(TAPS)
            ]
            out[row * part : (row + 1) * part, start : start + TAPS * width] = jnp.concatenate(
                pieces, axis=1
            )
    square = (part, part)
    diagonal = lax.broadcasted_iota(jnp.int32, square, 0) == lax.broadcasted_iota(jnp.int32, square, 1)
    lane = lax.broadcasted_iota(jnp.int32, (part, LANES), 1)
    block = jnp.zeros((part, LANES), jnp.float32)
    for index, bias in enumerate(biases):
        rest = bias[...]
        for piece in range(PIECES):
            rounded = rest.astype(jnp.bfloat16).astype(jnp.float32)
            rest = rest - rounded
            spread = jnp.broadcast_to(rounded, square)
            column = jnp.sum(jnp.where(diagonal, spread, 0.0), axis=1, keepdims=True)
            block = jnp.where(lane == PIECES * index + piece, column, block)
    out[:part, end:] = block.astype(jnp.bfloat16)
    out[part:, end:] = jnp.zeros(((TAPS - 1) * part, LANES), jnp.bfloat16)


def moved(value, step):
    cols = value.shape[1]
    lane = lax.broadcasted_iota(jnp.int32, value.shape, 1)
    rolled = pltpu.roll(value, lax.rem(cols - step, cols), 1)
    return jnp.where((lane + step >= 0) & (lane + step < cols), rolled, jnp.zeros_like(rolled))


def taps(value):
    return jnp.concatenate([moved(value, -1), value, moved(value, 1)], axis=0)


def recurrence(sizes, widths, *refs):
    frames, tiles, chans, segments, part, depth, cols = sizes
    span, groups, count = split_of(segments, tiles)
    n_blocks = frames * tiles * chans
    sides, refs = refs[:chans], refs[chans:]
    blocks, refs = refs[:n_blocks], refs[n_blocks:]
    outs, refs = refs[:groups], refs[groups:]
    weights, numbers, table, features, joined, inner, history, stage = refs[:8]
    fetched, arrived, counted = refs[8:]
    channels = part * chans
    rows = tiles * depth
    tile, frame_here, chan = (lax.axis_index(name) for name in ("tiles", "frames", "chan"))
    kept = history.shape[0]
    top = depth + 1
    starts = starts_of(widths)

    def copy_in(segment, shift, index):
        frame = origin(frame_here, shift, frames)
        source_tile = origin(tile, index // chans, tiles)
        source_chan = origin(chan, index % chans, chans)
        return pltpu.make_async_copy(
            blocks[shift * tiles * chans + index].at[segment],
            features.at[frame, source_chan, source_tile],
            arrived.at[shift, index],
        )

    def every_copy(segment):
        for shift in range(frames):
            for index in range(tiles * chans):
                yield copy_in(segment, shift, index)

    def weight_copies():
        for side in range(chans):
            place = pl.multiple_of(origin(chan, side, chans) * part, part)
            for row in range(TAPS):
                yield pltpu.make_async_copy(
                    sides[side].at[pl.ds(row * part, part)],
                    weights.at[pl.ds(row * channels + place, part)],
                    fetched.at[side, row],
                )

    def bias_of(index):
        block = weights[:channels, starts[-1] : starts[-1] + LANES].astype(jnp.float32)
        lane = lax.broadcasted_iota(jnp.int32, block.shape, 1)
        mine = (lane >= PIECES * index) & (lane < PIECES * (index + 1))
        column = jnp.sum(jnp.where(mine, block, 0.0), axis=1, keepdims=True)
        return jnp.broadcast_to(column, (channels, cols))

    def convolve(inputs, index, emit):
        low = starts[index]
        matrix = weights[:, low : low + TAPS * channels * len(inputs)]
        bias = bias_of(index)

        def step(block, carried):
            above, here = carried
            slabs = [
                jnp.concatenate([taps(load(block, row)) for load in inputs], axis=0)
                for row in range(depth)
            ]
            partial = jnp.dot(
                matrix, jnp.concatenate(slabs, axis=1), preferred_element_type=jnp.float32
            )
            for row in range(depth):
                one = partial[:, row * cols : (row + 1) * cols]
                emit(block * depth + row, above + one[2 * channels :])
                above = here + one[channels : 2 * channels]
                here = bias + one[:channels]
            return above, here

        unroll = UNROLL if tiles % UNROLL == 0 else 1
        above, _ = lax.fori_loop(0, tiles, step, (bias, bias), unroll=unroll)
        emit(rows, above)

    def stored(ref):
        return lambda block, row: ref[block * depth + row + 1]

    def displaced(held, field):
        def load(block, row):
            down = table[block, field]
            right = table[block, field + 1]
            return moved(held[top + block * depth + row + down], right)

        return load

    for copy in weight_copies():
        copy.start()
    for segment in range(count):
        for copy in every_copy(segment):
            copy.start()
        if segment == 0:
            for index in range(kept):
                history[index, :top] = jnp.zeros((top, channels, cols), jnp.bfloat16)
                history[index, top + rows :] = jnp.zeros((depth, channels, cols), jnp.bfloat16)
            for copy in weight_copies():
                copy.wait()
        for copy in every_copy(segment):
            copy.wait()
        for block in range(tiles):
            tail = features[0, 0, block, part * depth :].astype(jnp.float32).astype(jnp.int32)
            numbers[block : block + 1, :] = tail[:1]
        to_table = pltpu.make_async_copy(numbers, table, counted)
        to_table.start()
        for frame in range(frames):
            def load_own(block, row, frame=frame):
                pieces = [
                    features[frame, side, block, row * part : (row + 1) * part]
                    for side in range(chans)
                ]
                return jnp.concatenate(pieces, axis=0)

            inputs = [load_own]
            for back, field in ((1, 2 * frame), (2, 2 * (frames + frame))):
                if frame >= back:
                    inputs.append(displaced(history.at[(frame - back) % kept], field))
            if frame == min(1, frames - 1):
                to_table.wait()
            new = history.at[frame % kept]

            def emit_join(slot, total):
                joined[slot] = jnp.where(total > 0, total, 0.1 * total).astype(jnp.bfloat16)

            def emit_inner(slot, total):
                inner[slot] = jnp.maximum(total, 0.0).astype(jnp.bfloat16)

            def emit_second(slot, total, new=new):
                state = joined[slot].astype(jnp.float32) + total
                new[top - 1 + slot] = state.astype(jnp.bfloat16)

            convolve(inputs, 0, emit_join)
            convolve([stored(joined)], 1, emit_inner)
            convolve([stored(inner)], 2, emit_second)
            new[top - 1] = jnp.zeros((channels, cols), jnp.bfloat16)

            @pl.when(frame_here == frame)
            def _(segment=segment, new=new):
                for turn in range(groups):
                    target = partner(tile // span, turn, groups) * span + lax.rem(tile, span)
                    for row in range(depth):
                        value = new[
                            top + target * depth + row, pl.ds(pl.multiple_of(chan * part, part), part)
                        ]
                        stage[turn, pl.ds(row, part, stride=depth), :] = value.astype(jnp.float32)
                    whole = stage[turn].reshape(part, depth, cols)
                    outs[turn][segment] = whole.astype(jnp.bfloat16)


def shards(lr_feats, flow_prev, flow_second, w_join, b_join, w_first, b_first, w_second, b_second):
    segments, _, part, depth, cols = lr_feats.shape
    frames, tiles, chans = (lax.axis_size(name) for name in ("frames", "tiles", "chan"))
    span, groups, count = split_of(segments, tiles)
    channels = part * chans
    rows = tiles * depth
    kept = min(frames, 3)
    tall = part * depth + TAIL
    slots = tiles * count

    flows = [flow.transpose(1, 2, 3, 0) for flow in (flow_prev, flow_second)]
    packed = call(
        pack,
        in_hbm(lr_feats, *flows),
        [jax.ShapeDtypeStruct((count, tall, cols), jnp.bfloat16)] * tiles,
        [
            pltpu.VMEM((slots, part, depth, cols), jnp.bfloat16),
            pltpu.SMEM(flows[0].shape, jnp.int32),
            pltpu.SMEM(flows[1].shape, jnp.int32),
            pltpu.VMEM((slots, part * depth, cols), jnp.float32),
            pltpu.SemaphoreType.DMA((slots + 2,)),
        ],
        [HBM] * 3,
        [VMEM] * tiles,
    )

    widths = (w_join.shape[2], w_first.shape[3], w_second.shape[3])
    wide = starts_of(widths)[-1] + LANES
    own = {0: packed[0]}
    for shift in ranked(tiles):
        own[shift] = hop(packed[shift], "tiles", shift)
    params = (w_join, w_first[0], w_second[0], b_join[None], b_first, b_second)
    arranged = call(
        functools.partial(arrange, widths),
        in_hbm(*params),
        jax.ShapeDtypeStruct((TAPS * part, wide), jnp.bfloat16),
        [pltpu.VMEM(item.shape, item.dtype) for item in params]
        + [pltpu.SemaphoreType.DMA((len(params),))],
        [HBM] * len(params),
        VMEM,
    )
    sides = [hop(arranged, "chan", side) for side in range(chans)]

    blocks = []
    for turn in range(frames):
        for shift in range(tiles):
            block = hop(own[shift], "frames", turn)
            blocks += [hop(block, "chan", side) for side in range(chans)]

    outs = call(
        functools.partial(recurrence, (frames, tiles, chans, segments, part, depth, cols), widths),
        (*sides, *blocks),
        [jax.ShapeDtypeStruct((count, part, depth, cols), jnp.bfloat16)] * groups,
        [
            pltpu.VMEM((TAPS * channels, wide), jnp.bfloat16),
            pltpu.VMEM((tiles, cols), jnp.int32),
            pltpu.SMEM((tiles, cols), jnp.int32),
            pltpu.VMEM((frames, chans, tiles, tall, cols), jnp.bfloat16),
            pltpu.VMEM((rows + 1, channels, cols), jnp.bfloat16),
            pltpu.VMEM((rows + 1, channels, cols), jnp.bfloat16),
            pltpu.VMEM((kept, rows + 2 * depth + 1, channels, cols), jnp.bfloat16),
            pltpu.VMEM((groups, part * depth, cols), jnp.float32),
            pltpu.SemaphoreType.DMA((chans, TAPS)),
            pltpu.SemaphoreType.DMA((frames, tiles * chans)),
            pltpu.SemaphoreType.DMA(()),
        ],
        [VMEM] * (chans + len(blocks)),
        [VMEM] * groups,
    )
    returned = {0: outs[0]}
    for turn in ranked(groups):
        returned[turn] = hop(outs[turn], "tiles", turn, span)
    return call(
        unpack,
        tuple(returned[turn] for turn in range(groups)),
        jax.ShapeDtypeStruct(lr_feats.shape, lr_feats.dtype),
        [pltpu.SemaphoreType.DMA((segments,))],
        [VMEM] * groups,
        HBM,
    )


def solution(mesh):
    in_specs = (
        P("clips", "frames", "chan", "tiles", None),
        P("clips", None, "tiles", None),
        P("clips", None, "tiles", None),
        P(None, "chan", None),
        P("chan"),
        P(None, None, "chan", None),
        P(None, "chan"),
        P(None, None, "chan", None),
        P(None, "chan"),
    )
    out_specs = P("clips", "frames", "chan", "tiles", None)
    return jax.shard_map(
        shards,
        mesh=mesh,
        in_specs=in_specs,
        out_specs=out_specs,
        check_vma=False,
    )
```

```python
import functools
import math

import jax
import jax.numpy as jnp
from jax import lax
from jax.experimental import pallas as pl
from jax.experimental.pallas import tpu as pltpu
from jax.sharding import PartitionSpec as P


TAPS = 3
LANES = 128
TAIL = 8
PIECES = 3
UNROLL = 8
GROUP = 4
SPARE = 4 * 2**20
VMEM = pl.BlockSpec(memory_space=pltpu.VMEM)
HBM = pl.BlockSpec(memory_space=pltpu.HBM)


def partner(index, shift, count):
    return (index + shift) % count if isinstance(index, int) else lax.rem(index + shift, count)


def origin(index, shift, count):
    return lax.rem(index + count - shift, count)


def hop(array, axis, shift, stride=1):
    count = lax.axis_size(axis) // stride
    if shift == 0:
        return array
    pairs = [
        (i * stride + j, partner(i, shift, count) * stride + j)
        for i in range(count)
        for j in range(stride)
    ]
    return lax.ppermute(array, axis, pairs)


def ranked(count):
    return list(range(1, count))


def in_hbm(*arrays):
    return tuple(pltpu.with_memory_space_constraint(array, pltpu.HBM) for array in arrays)


def call(kernel, operands, out_shape, scratch, in_specs, out_specs):
    shapes = jax.tree.leaves((operands, out_shape))
    held = sum(
        shape.size * shape.dtype.itemsize
        for shape in shapes
    ) + sum(
        math.prod(item.shape) * jnp.dtype(item.dtype).itemsize
        for item in scratch
        if item.memory_space == pltpu.VMEM
    )
    return pl.pallas_call(
        kernel,
        out_shape=out_shape,
        in_specs=in_specs,
        out_specs=out_specs,
        scratch_shapes=scratch,
        compiler_params=pltpu.CompilerParams(vmem_limit_bytes=held + SPARE),
    )(*operands)


def split_of(segments, tiles):
    span = max(1, tiles // segments)
    groups = tiles // span
    return span, groups, segments // groups


def starts_of(widths):
    starts, at = [], 0
    for width in widths:
        starts.append(at)
        at += -(-TAPS * width // LANES) * LANES
    return starts + [at]


def pack(lr_feats, *rest):
    flows, rest = rest[:2], rest[2:]
    outs, rest = rest[:-5], rest[-5:]
    held, table_prev, table_second, stage, came = rest
    segments, _, part, depth, cols = lr_feats.shape
    frames = flows[0].shape[0]
    tiles = len(outs)
    span, _, count = split_of(segments, tiles)
    tile = lax.axis_index("tiles")
    tables = (table_prev, table_second)
    fetches = [
        pltpu.make_async_copy(flow, table, came.at[len(outs) * count + index])
        for index, (flow, table) in enumerate(zip(flows, tables))
    ]
    order = ranked(tiles) + [0]

    def first_of(shift):
        return partner(tile, shift, tiles) // span * count

    loads = {}
    for shift in order:
        for index in range(count):
            slot = shift * count + index
            loads[slot] = pltpu.make_async_copy(
                lr_feats.at[first_of(shift) + index, 0], held.at[slot], came.at[slot]
            )
            loads[slot].start()
    for fetch in fetches:
        fetch.start()
    lane = lax.broadcasted_iota(jnp.int32, (TAIL, cols), 1)
    for shift in order:
        for index in range(count):
            slot = shift * count + index
            loads[slot].wait()
            stage[slot] = held[slot].astype(jnp.float32).reshape(part * depth, cols)
            for row in range(depth):
                value = stage[slot, pl.ds(row, part, stride=depth), :]
                outs[shift][index, row * part : (row + 1) * part] = value.astype(jnp.bfloat16)
    for fetch in fetches:
        fetch.wait()
    for shift in order:
        for index in range(count):
            tail = jnp.zeros((TAIL, cols), jnp.int32)
            for which, table in enumerate(tables):
                for frame in range(frames):
                    for entry in range(2):
                        at = (which * frames + frame) * 2 + entry
                        number = table[frame, 0, entry, first_of(shift) + index]
                        tail = jnp.where(lane == at, number, tail)
            outs[shift][index, part * depth :] = tail.astype(jnp.float32).astype(jnp.bfloat16)


def unpack(*refs):
    blocks, out, left = refs[:-2], refs[-2], refs[-1]
    groups = len(blocks)
    count = out.shape[0] // groups
    span = lax.axis_size("tiles") // groups
    tile = lax.axis_index("tiles")
    copies = []
    for turn, block in enumerate(blocks):
        first = origin(tile // span, turn, groups) * count
        for index in range(count):
            copies.append(
                pltpu.make_async_copy(
                    block.at[index], out.at[first + index, 0], left.at[turn * count + index]
                )
            )
    for copy in copies:
        copy.start()
    for copy in copies:
        copy.wait()


def arrange(widths, *refs):
    count = len(widths)
    sources, out, rest = refs[: 2 * count], refs[2 * count], refs[2 * count + 1 :]
    copies = [
        pltpu.make_async_copy(source, held, rest[-1].at[index])
        for index, (source, held) in enumerate(zip(sources, rest))
    ]
    for copy in copies:
        copy.start()
    for copy in copies:
        copy.wait()
    weights, biases = rest[:count], rest[count : 2 * count]
    part = out.shape[0] // TAPS
    *starts, end = starts_of(widths)
    channels = min(widths)
    for weight, width, start in zip(weights, widths, starts):
        for row in range(TAPS):
            pieces = [
                weight[TAPS * row + col, :, source : source + channels]
                for source in range(0, width, channels)
                for col in range(TAPS)
            ]
            out[row * part : (row + 1) * part, start : start + TAPS * width] = jnp.concatenate(
                pieces, axis=1
            )
    square = (part, part)
    diagonal = lax.broadcasted_iota(jnp.int32, square, 0) == lax.broadcasted_iota(jnp.int32, square, 1)
    lane = lax.broadcasted_iota(jnp.int32, (part, LANES), 1)
    block = jnp.zeros((part, LANES), jnp.float32)
    for index, bias in enumerate(biases):
        rest = bias[...]
        for piece in range(PIECES):
            rounded = rest.astype(jnp.bfloat16).astype(jnp.float32)
            rest = rest - rounded
            spread = jnp.broadcast_to(rounded, square)
            column = jnp.sum(jnp.where(diagonal, spread, 0.0), axis=1, keepdims=True)
            block = jnp.where(lane == PIECES * index + piece, column, block)
    out[:part, end:] = block.astype(jnp.bfloat16)
    out[part:, end:] = jnp.zeros(((TAPS - 1) * part, LANES), jnp.bfloat16)


def moved(value, step):
    cols = value.shape[1]
    lane = lax.broadcasted_iota(jnp.int32, value.shape, 1)
    rolled = pltpu.roll(value, lax.rem(cols - step, cols), 1)
    return jnp.where((lane + step >= 0) & (lane + step < cols), rolled, jnp.zeros_like(rolled))


def taps(value):
    return jnp.concatenate([moved(value, -1), value, moved(value, 1)], axis=0)


def recurrence(sizes, widths, *refs):
    frames, tiles, chans, segments, part, depth, cols = sizes
    span, groups, count = split_of(segments, tiles)
    n_blocks = frames * tiles * chans
    sides, refs = refs[:chans], refs[chans:]
    blocks, refs = refs[:n_blocks], refs[n_blocks:]
    outs, refs = refs[:groups], refs[groups:]
    weights, numbers, table, features, joined, inner, history, stage, counted = refs
    channels = part * chans
    rows = tiles * depth
    tile, frame_here, chan = (lax.axis_index(name) for name in ("tiles", "frames", "chan"))
    kept = history.shape[0]
    top = depth + 1
    starts = starts_of(widths)

    def place_blocks(segment):
        for shift in range(frames):
            frame = origin(frame_here, shift, frames)
            for index in range(tiles * chans):
                source_tile = origin(tile, index // chans, tiles)
                source_chan = origin(chan, index % chans, chans)
                block = blocks[shift * tiles * chans + index]
                features[frame, source_chan, source_tile] = block[segment]

    def place_weights():
        for side in range(chans):
            place = pl.multiple_of(origin(chan, side, chans) * part, part)
            for row in range(TAPS):
                weights[pl.ds(row * channels + place, part)] = sides[side][
                    row * part : (row + 1) * part
                ]

    def bias_of(index):
        block = weights[:channels, starts[-1] : starts[-1] + LANES].astype(jnp.float32)
        lane = lax.broadcasted_iota(jnp.int32, block.shape, 1)
        mine = (lane >= PIECES * index) & (lane < PIECES * (index + 1))
        column = jnp.sum(jnp.where(mine, block, 0.0), axis=1, keepdims=True)
        return jnp.broadcast_to(column, (channels, cols))

    def convolve(inputs, index, emit):
        low = starts[index]
        matrix = weights[:, low : low + TAPS * channels * len(inputs)]
        bias = bias_of(index)

        def step(turn, carried):
            above, here = carried
            first = turn * GROUP
            block = lax.div(first, depth)
            slabs = [
                jnp.concatenate([taps(load(block, first + row)) for load in inputs], axis=0)
                for row in range(GROUP)
            ]
            partial = jnp.dot(
                matrix, jnp.concatenate(slabs, axis=1), preferred_element_type=jnp.float32
            )
            for row in range(GROUP):
                one = partial[:, row * cols : (row + 1) * cols]
                emit(first + row, above + one[2 * channels :])
                above = here + one[channels : 2 * channels]
                here = bias + one[:channels]
            return above, here

        turns = rows // GROUP
        above, _ = lax.fori_loop(0, turns, step, (bias, bias), unroll=math.gcd(turns, UNROLL))
        emit(rows, above)

    def stored(ref):
        return lambda block, row: ref[row + 1]

    def displaced(held, field):
        def load(block, row):
            down = table[block, field]
            right = table[block, field + 1]
            return moved(held[top + row + down], right)

        return load

    place_weights()
    for index in range(kept):
        history[index, :top] = jnp.zeros((top, channels, cols), jnp.bfloat16)
        history[index, top + rows :] = jnp.zeros((depth, channels, cols), jnp.bfloat16)
    for segment in range(count):
        place_blocks(segment)
        for block in range(tiles):
            tail = features[0, 0, block, part * depth :].astype(jnp.float32).astype(jnp.int32)
            numbers[block : block + 1, :] = tail[:1]
        to_table = pltpu.make_async_copy(numbers, table, counted)
        to_table.start()
        for frame in range(frames):
            def load_own(block, row, frame=frame):
                first = pl.multiple_of(lax.rem(row, depth) * part, part)
                pieces = [features[frame, side, block, pl.ds(first, part)] for side in range(chans)]
                return jnp.concatenate(pieces, axis=0)

            inputs = [load_own]
            for back, field in ((1, 2 * frame), (2, 2 * (frames + frame))):
                if frame >= back:
                    inputs.append(displaced(history.at[(frame - back) % kept], field))
            if frame == min(1, frames - 1):
                to_table.wait()
            new = history.at[frame % kept]

            def emit_join(slot, total):
                joined[slot] = jnp.where(total > 0, total, 0.1 * total).astype(jnp.bfloat16)

            def emit_inner(slot, total):
                inner[slot] = jnp.maximum(total, 0.0).astype(jnp.bfloat16)

            def emit_second(slot, total, new=new):
                state = joined[slot].astype(jnp.float32) + total
                new[top - 1 + slot] = state.astype(jnp.bfloat16)

            convolve(inputs, 0, emit_join)
            convolve([stored(joined)], 1, emit_inner)
            convolve([stored(inner)], 2, emit_second)
            new[top - 1] = jnp.zeros((channels, cols), jnp.bfloat16)

            @pl.when(frame_here == frame)
            def _(segment=segment, new=new):
                for turn in range(groups):
                    target = partner(tile // span, turn, groups) * span + lax.rem(tile, span)
                    for row in range(depth):
                        value = new[
                            top + target * depth + row, pl.ds(pl.multiple_of(chan * part, part), part)
                        ]
                        stage[turn, pl.ds(row, part, stride=depth), :] = value.astype(jnp.float32)
                    whole = stage[turn].reshape(part, depth, cols)
                    outs[turn][segment] = whole.astype(jnp.bfloat16)


def shards(lr_feats, flow_prev, flow_second, w_join, b_join, w_first, b_first, w_second, b_second):
    segments, _, part, depth, cols = lr_feats.shape
    frames, tiles, chans = (lax.axis_size(name) for name in ("frames", "tiles", "chan"))
    span, groups, count = split_of(segments, tiles)
    channels = part * chans
    rows = tiles * depth
    kept = min(frames, 3)
    tall = part * depth + TAIL
    slots = tiles * count

    flows = [flow.transpose(1, 2, 3, 0) for flow in (flow_prev, flow_second)]
    packed = call(
        pack,
        in_hbm(lr_feats, *flows),
        [jax.ShapeDtypeStruct((count, tall, cols), jnp.bfloat16)] * tiles,
        [
            pltpu.VMEM((slots, part, depth, cols), jnp.bfloat16),
            pltpu.SMEM(flows[0].shape, jnp.int32),
            pltpu.SMEM(flows[1].shape, jnp.int32),
            pltpu.VMEM((slots, part * depth, cols), jnp.float32),
            pltpu.SemaphoreType.DMA((slots + 2,)),
        ],
        [HBM] * 3,
        [VMEM] * tiles,
    )

    widths = (w_join.shape[2], w_first.shape[3], w_second.shape[3])
    wide = starts_of(widths)[-1] + LANES
    own = {0: packed[0]}
    for shift in ranked(tiles):
        own[shift] = hop(packed[shift], "tiles", shift)
    params = (w_join, w_first[0], w_second[0], b_join[None], b_first, b_second)
    arranged = call(
        functools.partial(arrange, widths),
        in_hbm(*params),
        jax.ShapeDtypeStruct((TAPS * part, wide), jnp.bfloat16),
        [pltpu.VMEM(item.shape, item.dtype) for item in params]
        + [pltpu.SemaphoreType.DMA((len(params),))],
        [HBM] * len(params),
        VMEM,
    )
    sides = [hop(arranged, "chan", side) for side in range(chans)]

    blocks = []
    for turn in range(frames):
        for shift in range(tiles):
            block = hop(own[shift], "frames", turn)
            blocks += [hop(block, "chan", side) for side in range(chans)]

    outs = call(
        functools.partial(recurrence, (frames, tiles, chans, segments, part, depth, cols), widths),
        (*sides, *blocks),
        [jax.ShapeDtypeStruct((count, part, depth, cols), jnp.bfloat16)] * groups,
        [
            pltpu.VMEM((TAPS * channels, wide), jnp.bfloat16),
            pltpu.VMEM((tiles, cols), jnp.int32),
            pltpu.SMEM((tiles, cols), jnp.int32),
            pltpu.VMEM((frames, chans, tiles, tall, cols), jnp.bfloat16),
            pltpu.VMEM((rows + 1, channels, cols), jnp.bfloat16),
            pltpu.VMEM((rows + 1, channels, cols), jnp.bfloat16),
            pltpu.VMEM((kept, rows + 2 * depth + 1, channels, cols), jnp.bfloat16),
            pltpu.VMEM((groups, part * depth, cols), jnp.float32),
            pltpu.SemaphoreType.DMA(()),
        ],
        [VMEM] * (chans + len(blocks)),
        [VMEM] * groups,
    )
    returned = {0: outs[0]}
    for turn in ranked(groups):
        returned[turn] = hop(outs[turn], "tiles", turn, span)
    return call(
        unpack,
        tuple(returned[turn] for turn in range(groups)),
        jax.ShapeDtypeStruct(lr_feats.shape, lr_feats.dtype),
        [pltpu.SemaphoreType.DMA((segments,))],
        [VMEM] * groups,
        HBM,
    )


def solution(mesh):
    in_specs = (
        P("clips", "frames", "chan", "tiles", None),
        P("clips", None, "tiles", None),
        P("clips", None, "tiles", None),
        P(None, "chan", None),
        P("chan"),
        P(None, None, "chan", None),
        P(None, "chan"),
        P(None, None, "chan", None),
        P(None, "chan"),
    )
    out_specs = P("clips", "frames", "chan", "tiles", None)
    return jax.shard_map(
        shards,
        mesh=mesh,
        in_specs=in_specs,
        out_specs=out_specs,
        check_vma=False,
    )
```

```python
import functools
import math

import jax
import jax.numpy as jnp
from jax import lax
from jax.experimental import pallas as pl
from jax.experimental.pallas import tpu as pltpu
from jax.sharding import PartitionSpec as P


TAPS = 3
LANES = 128
TAIL = 8
PIECES = 3
UNROLL = 8
GROUP = 4
SPARE = 4 * 2**20
VMEM = pl.BlockSpec(memory_space=pltpu.VMEM)
HBM = pl.BlockSpec(memory_space=pltpu.HBM)


def partner(index, shift, count):
    return (index + shift) % count if isinstance(index, int) else lax.rem(index + shift, count)


def origin(index, shift, count):
    return lax.rem(index + count - shift, count)


def hop(array, axis, shift, stride=1):
    count = lax.axis_size(axis) // stride
    if shift == 0:
        return array
    pairs = [
        (i * stride + j, partner(i, shift, count) * stride + j)
        for i in range(count)
        for j in range(stride)
    ]
    return lax.ppermute(array, axis, pairs)


def ranked(count):
    return list(range(1, count))


def in_hbm(*arrays):
    return tuple(pltpu.with_memory_space_constraint(array, pltpu.HBM) for array in arrays)


def call(kernel, operands, out_shape, scratch, in_specs, out_specs, aliases=None):
    shapes = jax.tree.leaves((operands, out_shape))
    held = sum(
        shape.size * shape.dtype.itemsize
        for shape in shapes
    ) + sum(
        math.prod(item.shape) * jnp.dtype(item.dtype).itemsize
        for item in scratch
        if item.memory_space == pltpu.VMEM
    )
    return pl.pallas_call(
        kernel,
        out_shape=out_shape,
        in_specs=in_specs,
        out_specs=out_specs,
        scratch_shapes=scratch,
        input_output_aliases=aliases or {},
        compiler_params=pltpu.CompilerParams(vmem_limit_bytes=held + SPARE),
    )(*operands)


def split_of(segments, tiles):
    span = max(1, tiles // segments)
    groups = tiles // span
    return span, groups, segments // groups


def starts_of(widths):
    starts, at = [], 0
    for width in widths:
        starts.append(at)
        at += -(-TAPS * width // LANES) * LANES
    return starts + [at]


def pack(lr_feats, *rest):
    flows, rest = rest[:2], rest[2:]
    outs, rest = rest[:-5], rest[-5:]
    held, table_prev, table_second, stage, came = rest
    segments, _, part, depth, cols = lr_feats.shape
    frames = flows[0].shape[0]
    tiles = len(outs)
    span, _, count = split_of(segments, tiles)
    tile = lax.axis_index("tiles")
    tables = (table_prev, table_second)
    fetches = [
        pltpu.make_async_copy(flow, table, came.at[len(outs) * count + index])
        for index, (flow, table) in enumerate(zip(flows, tables))
    ]
    order = ranked(tiles) + [0]

    def first_of(shift):
        return partner(tile, shift, tiles) // span * count

    loads = {}
    for shift in order:
        for index in range(count):
            slot = shift * count + index
            loads[slot] = pltpu.make_async_copy(
                lr_feats.at[first_of(shift) + index, 0], held.at[slot], came.at[slot]
            )
            loads[slot].start()
    for fetch in fetches:
        fetch.start()
    lane = lax.broadcasted_iota(jnp.int32, (TAIL, cols), 1)
    for shift in order:
        for index in range(count):
            slot = shift * count + index
            loads[slot].wait()
            stage[slot] = held[slot].astype(jnp.float32).reshape(part * depth, cols)
            for row in range(depth):
                value = stage[slot, pl.ds(row, part, stride=depth), :]
                outs[shift][index, row * part : (row + 1) * part] = value.astype(jnp.bfloat16)
    for fetch in fetches:
        fetch.wait()
    for shift in order:
        for index in range(count):
            tail = jnp.zeros((TAIL, cols), jnp.int32)
            for which, table in enumerate(tables):
                for frame in range(frames):
                    for entry in range(2):
                        at = (which * frames + frame) * 2 + entry
                        number = table[frame, 0, entry, first_of(shift) + index]
                        tail = jnp.where(lane == at, number, tail)
            outs[shift][index, part * depth :] = tail.astype(jnp.float32).astype(jnp.bfloat16)


def unpack(turns, groups, *refs):
    blocks, (out, stage, ready, left) = refs[: len(turns)], refs[-4:]
    count, depth, part, cols = blocks[0].shape
    tile = lax.axis_index("tiles")
    span = lax.axis_size("tiles") // groups
    copies = []
    for place, (turn, block) in enumerate(zip(turns, blocks)):
        first = origin(tile // span, turn, groups) * count
        for index in range(count):
            slot = place * count + index
            for row in range(depth):
                value = block[index, row].astype(jnp.float32)
                stage[slot, pl.ds(row, part, stride=depth), :] = value
            ready[slot] = stage[slot].reshape(part, depth, cols).astype(jnp.bfloat16)
            copy = pltpu.make_async_copy(ready.at[slot], out.at[first + index, 0], left.at[slot])
            copy.start()
            copies.append(copy)
    for copy in copies:
        copy.wait()


def arrange(widths, *refs):
    count = len(widths)
    sources, out, rest = refs[: 2 * count], refs[2 * count], refs[2 * count + 1 :]
    copies = [
        pltpu.make_async_copy(source, held, rest[-1].at[index])
        for index, (source, held) in enumerate(zip(sources, rest))
    ]
    for copy in copies:
        copy.start()
    for copy in copies:
        copy.wait()
    weights, biases = rest[:count], rest[count : 2 * count]
    part = out.shape[0] // TAPS
    *starts, end = starts_of(widths)
    channels = min(widths)
    for weight, width, start in zip(weights, widths, starts):
        for row in range(TAPS):
            pieces = [
                weight[TAPS * row + col, :, source : source + channels]
                for source in range(0, width, channels)
                for col in range(TAPS)
            ]
            out[row * part : (row + 1) * part, start : start + TAPS * width] = jnp.concatenate(
                pieces, axis=1
            )
    square = (part, part)
    diagonal = lax.broadcasted_iota(jnp.int32, square, 0) == lax.broadcasted_iota(jnp.int32, square, 1)
    lane = lax.broadcasted_iota(jnp.int32, (part, LANES), 1)
    block = jnp.zeros((part, LANES), jnp.float32)
    for index, bias in enumerate(biases):
        rest = bias[...]
        for piece in range(PIECES):
            rounded = rest.astype(jnp.bfloat16).astype(jnp.float32)
            rest = rest - rounded
            spread = jnp.broadcast_to(rounded, square)
            column = jnp.sum(jnp.where(diagonal, spread, 0.0), axis=1, keepdims=True)
            block = jnp.where(lane == PIECES * index + piece, column, block)
    out[:part, end:] = block.astype(jnp.bfloat16)
    out[part:, end:] = jnp.zeros(((TAPS - 1) * part, LANES), jnp.bfloat16)


def moved(value, step):
    cols = value.shape[1]
    lane = lax.broadcasted_iota(jnp.int32, value.shape, 1)
    rolled = pltpu.roll(value, lax.rem(cols - step, cols), 1)
    return jnp.where((lane + step >= 0) & (lane + step < cols), rolled, jnp.zeros_like(rolled))


def taps(value):
    return jnp.concatenate([moved(value, -1), value, moved(value, 1)], axis=0)


def recurrence(sizes, widths, *refs):
    frames, tiles, chans, segments, part, depth, cols = sizes
    span, groups, count = split_of(segments, tiles)
    n_blocks = frames * tiles * chans
    sides, refs = refs[:chans], refs[chans:]
    blocks, refs = refs[:n_blocks], refs[n_blocks:]
    outs, refs = refs[:groups], refs[groups:]
    weights, numbers, table, features, joined, inner, history, final, counted = refs
    channels = part * chans
    rows = tiles * depth
    tile, frame_here, chan = (lax.axis_index(name) for name in ("tiles", "frames", "chan"))
    kept = history.shape[0]
    top = depth + 1
    starts = starts_of(widths)

    def place_blocks(segment):
        for shift in range(frames):
            frame = origin(frame_here, shift, frames)
            for index in range(tiles * chans):
                source_tile = origin(tile, index // chans, tiles)
                source_chan = origin(chan, index % chans, chans)
                block = blocks[shift * tiles * chans + index]
                features[frame, source_chan, source_tile] = block[segment]

    def place_weights():
        for side in range(chans):
            place = pl.multiple_of(origin(chan, side, chans) * part, part)
            for row in range(TAPS):
                weights[pl.ds(row * channels + place, part)] = sides[side][
                    row * part : (row + 1) * part
                ]

    def bias_of(matrix, index, many):
        block = matrix[:many, starts[-1] : starts[-1] + LANES].astype(jnp.float32)
        lane = lax.broadcasted_iota(jnp.int32, block.shape, 1)
        mine = (lane >= PIECES * index) & (lane < PIECES * (index + 1))
        column = jnp.sum(jnp.where(mine, block, 0.0), axis=1, keepdims=True)
        return jnp.broadcast_to(column, (many, cols))

    def convolve(inputs, index, emit, packed=weights):
        low = starts[index]
        many = packed.shape[0] // TAPS
        matrix = packed[:, low : low + TAPS * channels * len(inputs)]
        bias = bias_of(packed, index, many)

        def step(turn, carried):
            above, here = carried
            first = turn * GROUP
            block = lax.div(first, depth)
            slabs = [
                jnp.concatenate([taps(load(block, first + row)) for load in inputs], axis=0)
                for row in range(GROUP)
            ]
            partial = jnp.dot(
                matrix, jnp.concatenate(slabs, axis=1), preferred_element_type=jnp.float32
            )
            for row in range(GROUP):
                one = partial[:, row * cols : (row + 1) * cols]
                emit(first + row, above + one[2 * many :])
                above = here + one[many : 2 * many]
                here = bias + one[:many]
            return above, here

        turns = rows // GROUP
        above, _ = lax.fori_loop(0, turns, step, (bias, bias), unroll=math.gcd(turns, UNROLL))
        emit(rows, above)

    def stored(ref):
        return lambda block, row: ref[row + 1]

    def displaced(held, field):
        def load(block, row):
            down = table[block, field]
            right = table[block, field + 1]
            return moved(held[top + row + down], right)

        return load

    place_weights()
    for index in range(kept):
        history[index, :top] = jnp.zeros((top, channels, cols), jnp.bfloat16)
        history[index, top + rows :] = jnp.zeros((depth, channels, cols), jnp.bfloat16)
    for segment in range(count):
        place_blocks(segment)
        for block in range(tiles):
            tail = features[0, 0, block, part * depth :].astype(jnp.float32).astype(jnp.int32)
            numbers[block : block + 1, :] = tail[:1]
        to_table = pltpu.make_async_copy(numbers, table, counted)
        to_table.start()

        def run(frame, segment):
            def load_own(block, row):
                first = pl.multiple_of(lax.rem(row, depth) * part, part)
                pieces = [features[frame, side, block, pl.ds(first, part)] for side in range(chans)]
                return jnp.concatenate(pieces, axis=0)

            inputs = [load_own]
            for back, field in ((1, 2 * frame), (2, 2 * (frames + frame))):
                if frame >= back:
                    inputs.append(displaced(history.at[(frame - back) % kept], field))
            last = frame == frames - 1
            new = final if last else history.at[frame % kept]
            mine = pl.ds(pl.multiple_of(chan * part, part), part)

            def emit_join(slot, total):
                joined[slot] = jnp.where(total > 0, total, 0.1 * total).astype(jnp.bfloat16)

            def emit_inner(slot, total):
                inner[slot] = jnp.maximum(total, 0.0).astype(jnp.bfloat16)

            def emit_second(slot, total):
                before = joined[slot, mine] if last else joined[slot]
                new[top - 1 + slot] = (before.astype(jnp.float32) + total).astype(jnp.bfloat16)

            convolve(inputs, 0, emit_join)
            convolve([stored(joined)], 1, emit_inner)
            convolve([stored(inner)], 2, emit_second, sides[0] if last else weights)
            if not last:
                new[top - 1] = jnp.zeros((channels, cols), jnp.bfloat16)

            @pl.when(frame_here == frame)
            def _():
                for turn in range(groups):
                    target = partner(tile // span, turn, groups) * span + lax.rem(tile, span)
                    for row in range(depth):
                        at = top + target * depth + row
                        outs[turn][segment, row] = new[at] if last else new[at, mine]

        run(0, segment)
        to_table.wait()
        for frame in range(1, frames):
            pl.when(frame_here >= frame)(functools.partial(run, frame, segment))


def shards(lr_feats, flow_prev, flow_second, w_join, b_join, w_first, b_first, w_second, b_second):
    segments, _, part, depth, cols = lr_feats.shape
    frames, tiles, chans = (lax.axis_size(name) for name in ("frames", "tiles", "chan"))
    span, groups, count = split_of(segments, tiles)
    channels = part * chans
    rows = tiles * depth
    kept = min(frames, 3)
    tall = part * depth + TAIL
    slots = tiles * count

    flows = [flow.transpose(1, 2, 3, 0) for flow in (flow_prev, flow_second)]
    packed = call(
        pack,
        in_hbm(lr_feats, *flows),
        [jax.ShapeDtypeStruct((count, tall, cols), jnp.bfloat16)] * tiles,
        [
            pltpu.VMEM((slots, part, depth, cols), jnp.bfloat16),
            pltpu.SMEM(flows[0].shape, jnp.int32),
            pltpu.SMEM(flows[1].shape, jnp.int32),
            pltpu.VMEM((slots, part * depth, cols), jnp.float32),
            pltpu.SemaphoreType.DMA((slots + 2,)),
        ],
        [HBM] * 3,
        [VMEM] * tiles,
    )

    widths = (w_join.shape[2], w_first.shape[3], w_second.shape[3])
    wide = starts_of(widths)[-1] + LANES
    own = {0: packed[0]}
    for shift in ranked(tiles):
        own[shift] = hop(packed[shift], "tiles", shift)
    params = (w_join, w_first[0], w_second[0], b_join[None], b_first, b_second)
    arranged = call(
        functools.partial(arrange, widths),
        in_hbm(*params),
        jax.ShapeDtypeStruct((TAPS * part, wide), jnp.bfloat16),
        [pltpu.VMEM(item.shape, item.dtype) for item in params]
        + [pltpu.SemaphoreType.DMA((len(params),))],
        [HBM] * len(params),
        VMEM,
    )
    sides = [hop(arranged, "chan", side) for side in range(chans)]

    blocks = []
    for turn in range(frames):
        for shift in range(tiles):
            block = hop(own[shift], "frames", turn)
            blocks += [hop(block, "chan", side) for side in range(chans)]

    outs = call(
        functools.partial(recurrence, (frames, tiles, chans, segments, part, depth, cols), widths),
        (*sides, *blocks),
        [jax.ShapeDtypeStruct((count, depth, part, cols), jnp.bfloat16)] * groups,
        [
            pltpu.VMEM((TAPS * channels, wide), jnp.bfloat16),
            pltpu.VMEM((tiles, cols), jnp.int32),
            pltpu.SMEM((tiles, cols), jnp.int32),
            pltpu.VMEM((frames, chans, tiles, tall, cols), jnp.bfloat16),
            pltpu.VMEM((rows + 1, channels, cols), jnp.bfloat16),
            pltpu.VMEM((rows + 1, channels, cols), jnp.bfloat16),
            pltpu.VMEM((kept, rows + 2 * depth + 1, channels, cols), jnp.bfloat16),
            pltpu.VMEM((rows + 2 * depth + 1, part, cols), jnp.bfloat16),
            pltpu.SemaphoreType.DMA(()),
        ],
        [VMEM] * (chans + len(blocks)),
        [VMEM] * groups,
    )
    returned = {0: outs[0]}
    for turn in ranked(groups):
        returned[turn] = hop(outs[turn], "tiles", turn, span)
    turns = [0] + ranked(groups)
    result = ()
    for some in (turns[: groups // 2], turns[groups // 2 :]):
        if some:
            slots = len(some) * count
            result = (
                call(
                    functools.partial(unpack, some, groups),
                    tuple(returned[turn] for turn in some) + result,
                    jax.ShapeDtypeStruct(lr_feats.shape, lr_feats.dtype),
                    [
                        pltpu.VMEM((slots, part * depth, cols), jnp.float32),
                        pltpu.VMEM((slots, part, depth, cols), jnp.bfloat16),
                        pltpu.SemaphoreType.DMA((slots,)),
                    ],
                    [VMEM] * len(some) + [HBM] * len(result),
                    HBM,
                    {len(some): 0} if result else None,
                ),
            )
    return result[0]


def solution(mesh):
    in_specs = (
        P("clips", "frames", "chan", "tiles", None),
        P("clips", None, "tiles", None),
        P("clips", None, "tiles", None),
        P(None, "chan", None),
        P("chan"),
        P(None, None, "chan", None),
        P(None, "chan"),
        P(None, None, "chan", None),
        P(None, "chan"),
    )
    out_specs = P("clips", "frames", "chan", "tiles", None)
    return jax.shard_map(
        shards,
        mesh=mesh,
        in_specs=in_specs,
        out_specs=out_specs,
        check_vma=False,
    )
```
